256 devices in a mesh: grp: 8 (over z), pair: 32 (over x, y, core).
Axes of the slice: x: 4, y: 4, z: 8, core: 2. Of those that a mesh axis runs over, the one named last changes fastest.
Arguments:
- three_center: bfloat16 [512, 1024, 1024], P('pair', 'grp'), may hold values from -6 to 6
- virt_density: bfloat16 [1024, 1024], P(None, 'pair'), may hold values from -0.1875 to 0.1875
- occ_density: bfloat16 [1024, 1024], P(None, 'pair'), may hold values from -0.1875 to 0.1875
- tensor_mask: int32 [4, 8, 8], replicated, may hold values 0 or 1
- virt_mask: int32 [8, 8], replicated, may hold values 0 or 1
- occ_mask: int32 [8, 8], replicated, may hold values 0 or 1
- panel_order: int32 [512], replicated, may hold values from 0 to 511, each once
Outputs:
- response: float32 [512, 512], P(('grp', 'pair'))
The draws below stay inside these ranges and needn't reach their ends.
Inputs may be any that keep to these rules, and one draw needn't show every extreme that they name: `tensor_mask`: each block is 0 (absent) or 1 (present). `virt_mask`: each block is 0 (absent) or 1 (present). `occ_mask`: each block is 0 (absent) or 1 (present). `panel_order`: every auxiliary index appears exactly once.
All inputs are finite; a program needn't handle non-finite values.
Results may differ from the reference program's by a relative error of at most 0.0041.
Values may be sent and summed in bfloat16 or wider, within the bound.
No kernel may reach another device: no remote copies, remote signals or barrier semaphores. Data moves between devices by JAX's collectives and lax.ppermute only.
A program may use at most 128 MiB of HBM per device.

```python
import jax
import jax.numpy as jnp
from jax import lax

NAUX = 512
NORB = 1024
BLK = 128


def plant(entries, stream_key, smallest, high):
    index_at = [jax.random.randint(jax.random.fold_in(stream_key, axis), (), 0, length) for axis, length in enumerate(entries.shape)]
    widest = entries.shape.index(max(entries.shape))
    next_to = index_at[:widest] + [(index_at[widest] + 1) % entries.shape[widest]] + index_at[widest + 1:]
    return entries.at[tuple(index_at)].set(smallest).at[tuple(next_to)].set(high)


def steps_of(rng, extent, cuts, least, high):
    def one(position, parts):
        draws = jax.random.uniform(jax.random.fold_in(jax.random.fold_in(rng, 6), position), (parts,), jnp.float32, least / len(cuts), high / len(cuts))
        return jnp.repeat(jnp.exp(draws), extent[position] // parts).reshape((-1,) + (1,) * (len(extent) - position - 1))

    gain = one(*cuts[0])
    for cut in cuts[1:]:
        gain = gain * one(*cut)
    return gain


def scatter_about(own_key, shape, deviation, limit, pieces=(), kind=jnp.bfloat16):
    entries = deviation * jax.random.normal(own_key, shape, jnp.float32)
    if pieces:
        entries = entries * steps_of(own_key, shape, pieces, -0.22, 0.18)
    return jnp.clip(entries, -limit, limit).astype(kind)


def setup_inputs(seed: int = 0) -> dict:
    arg_keys = jax.random.split(jax.random.key(seed), 8)
    return {
        "three_center": scatter_about(arg_keys[0], (NAUX, NORB, NORB), 1.0, 6.0, ((0, 32), (1, 8))),
        "virt_density": scatter_about(arg_keys[1], (NORB, NORB), NORB ** -0.5, 0.1875, ((1, 32),)),
        "occ_density": scatter_about(arg_keys[2], (NORB, NORB), NORB ** -0.5, 0.1875, ((1, 32),)),
        "tensor_mask": plant((jax.random.randint(arg_keys[3], (NAUX // BLK, NORB // BLK, NORB // BLK), 0, 4) < 3).astype(jnp.int32), jax.random.fold_in(arg_keys[3], 1), 0, 1),
        "virt_mask": plant((jax.random.randint(arg_keys[4], (NORB // BLK, NORB // BLK), 0, 4) < 3).astype(jnp.int32), jax.random.fold_in(arg_keys[4], 1), 0, 1),
        "occ_mask": plant((jax.random.randint(arg_keys[5], (NORB // BLK, NORB // BLK), 0, 4) < 3).astype(jnp.int32), jax.random.fold_in(arg_keys[5], 1), 0, 1),
        "panel_order": jax.random.permutation(arg_keys[6], NAUX).astype(jnp.int32),
    }


def spread_blocks(table):
    return jnp.repeat(jnp.repeat(table, BLK, axis=0), BLK, axis=1)


def reference(three_center, virt_density, occ_density, tensor_mask, virt_mask, occ_mask, panel_order):
    virt_live = virt_density * spread_blocks(virt_mask).astype(jnp.bfloat16)
    occ_live = occ_density * spread_blocks(occ_mask).astype(jnp.bfloat16)

    def one_block(block_id):
        rows = lax.dynamic_slice_in_dim(three_center, block_id * BLK, BLK, 0)
        table = lax.dynamic_index_in_dim(tensor_mask, block_id, 0, keepdims=False)
        masked = rows * spread_blocks(table).astype(jnp.bfloat16)[None]
        half = jnp.dot(masked.reshape(BLK * NORB, NORB), virt_live, preferred_element_type=jnp.float32)
        half = half.astype(jnp.bfloat16).reshape(BLK, NORB, NORB)
        turned = jnp.transpose(half, (0, 2, 1)).reshape(BLK * NORB, NORB)
        trans = jnp.dot(turned, occ_live, preferred_element_type=jnp.float32).astype(jnp.bfloat16)
        return masked.reshape(BLK, NORB * NORB), trans.reshape(BLK, NORB * NORB)

    block_ids = jnp.arange(NAUX // BLK, dtype=jnp.int32)
    masked_all, trans_all = lax.map(one_block, block_ids)
    masked_all = masked_all.reshape(NAUX, NORB * NORB)
    trans_all = trans_all.reshape(NAUX, NORB * NORB)
    picked = jnp.take(trans_all, panel_order.astype(jnp.int32), axis=0)
    product = lax.dot_general(picked, masked_all, (((1,), (1,)), ((), ())), preferred_element_type=jnp.float32)
    return product * (1.0 / NORB)
```

```python
import functools

import jax
import jax.numpy as jnp
from jax import lax
from jax.experimental import pallas as pl
from jax.experimental.pallas import tpu as pltpu
from jax.sharding import PartitionSpec as P

NAUX = 512
NORB = 1024
BLK = 128
GRP = 8
PAIR = 32
AUX = NAUX // PAIR
SEC = NORB // GRP
COLS = NORB // PAIR
CHIPS = PAIR // 2
OWN = SEC // PAIR

SAME_CORE = [[core + 2 * chip for chip in range(CHIPS)] for core in range(2)]
PARTNER = [(i, i ^ 1) for i in range(PAIR)]
NT = (((1,), (1,)), ((), ()))
SMEM = pl.BlockSpec(memory_space=pltpu.SMEM)


def masked_rows(rows, keep):
    parts = []
    for b in range(NORB // BLK):
        part = rows[:, b * BLK : (b + 1) * BLK]
        parts.append(jnp.where(keep(b) != 0, part, jnp.zeros_like(part)))
    return jnp.concatenate(parts, axis=1)


S_TILE = 256


def half_kernel(place, virt_mask, tensor_mask, own, other, tensor, out, virt):
    core, table = place[0], place[1]
    tile = pl.program_id(0)
    chips = S_TILE // (2 * COLS)
    for c in range(chips):
        block = (tile * S_TILE + c * 2 * COLS) // BLK

        def keep(b):
            return virt_mask[b, block] * tensor_mask[table, b]

        mine = pl.multiple_of((2 * c + core) * COLS, COLS)
        theirs = pl.multiple_of((2 * c + 1 - core) * COLS, COLS)
        virt[pl.ds(mine, COLS), :] = masked_rows(own[c], keep)
        virt[pl.ds(theirs, COLS), :] = masked_rows(other[c], keep)
    half = lax.dot_general(virt[...], tensor[...], NT, preferred_element_type=jnp.float32)
    half = half.astype(jnp.bfloat16)
    by_aux = jnp.stack([half[:, a * SEC : (a + 1) * SEC] for a in range(AUX)], axis=0)
    out[...] = jnp.swapaxes(by_aux, 0, 1)


def half_transform(place, virt_mask, tensor_mask, own, other, tensor):
    chips = S_TILE // (2 * COLS)
    return pl.pallas_call(
        half_kernel,
        out_shape=jax.ShapeDtypeStruct((NORB, AUX, SEC), jnp.bfloat16),
        grid=(NORB // S_TILE,),
        in_specs=[
            SMEM,
            SMEM,
            SMEM,
            pl.BlockSpec((chips, COLS, NORB), lambda i: (i, 0, 0)),
            pl.BlockSpec((chips, COLS, NORB), lambda i: (i, 0, 0)),
            pl.BlockSpec((AUX * SEC, NORB), lambda i: (0, 0)),
        ],
        out_specs=pl.BlockSpec((S_TILE, AUX, SEC), lambda i: (i, 0, 0)),
        scratch_shapes=[pltpu.VMEM((S_TILE, NORB), jnp.bfloat16)],
        name="half_transform",
    )(place, virt_mask, tensor_mask, own, other, tensor)


M_TILE = 256


def turn_kernel(place, occ_mask, tensor_mask, own, other, tensor, out, occ):
    core, table = place[0], place[1]
    tile = pl.program_id(0)

    for c in range(CHIPS):
        block = c * 2 * COLS // BLK
        for rows, at in ((own, 2 * c + core), (other, 2 * c + 1 - core)):
            parts = []
            for b in range(M_TILE // BLK):
                part = rows[c, :, b * BLK : (b + 1) * BLK]
                live = occ_mask[tile * (M_TILE // BLK) + b, block] * tensor_mask[table, block]
                parts.append(jnp.where(live != 0, part, jnp.zeros_like(part)))
            occ[pl.ds(pl.multiple_of(at * COLS, COLS), COLS), :] = jnp.concatenate(parts, axis=1)

    turned = lax.dot_general(
        tensor[...], occ[...], (((1,), (0,)), ((), ())), preferred_element_type=jnp.float32
    )
    turned = turned.astype(jnp.bfloat16).reshape(AUX, SEC, M_TILE)
    out[...] = jnp.swapaxes(turned, 0, 1)


def turn_transform(place, occ_mask, tensor_mask, own, other, tensor):
    return pl.pallas_call(
        turn_kernel,
        out_shape=jax.ShapeDtypeStruct((SEC, AUX, NORB), jnp.bfloat16),
        grid=(NORB // M_TILE,),
        in_specs=[
            SMEM,
            SMEM,
            SMEM,
            pl.BlockSpec((CHIPS, COLS, M_TILE), lambda i: (0, 1, i)),
            pl.BlockSpec((CHIPS, COLS, M_TILE), lambda i: (0, 1, i)),
            pl.BlockSpec((AUX * SEC, NORB), lambda i: (0, 0)),
        ],
        out_specs=pl.BlockSpec((SEC, AUX, M_TILE), lambda i: (0, 0, i)),
        scratch_shapes=[pltpu.VMEM((NORB, M_TILE), jnp.bfloat16)],
        name="turn_transform",
    )(place, occ_mask, tensor_mask, own, other, tensor)


def response_kernel(order, left, right, out, total):
    step = pl.program_id(0)
    lhs = jnp.concatenate([left[g, :, 0].reshape(NAUX, SEC) for g in range(GRP)], axis=1)
    rhs = right[:, 0].reshape(NAUX, NORB)
    part = lax.dot_general(lhs, rhs, NT, preferred_element_type=jnp.float32)

    @pl.when(step == 0)
    def _():
        total[...] = part

    @pl.when(step > 0)
    def _():
        total[...] += part

    @pl.when(step == pl.num_programs(0) - 1)
    def _():
        rounded = (total[...] * (1.0 / NORB)).astype(jnp.bfloat16)
        columns = lax.broadcasted_iota(jnp.int32, (NAUX, NAUX), 1)
        pick = (order[...] == columns).astype(jnp.float32).astype(jnp.bfloat16)
        picked = jnp.dot(pick, rounded, preferred_element_type=jnp.float32)
        out[...] = picked.astype(jnp.bfloat16)


def partial_response(order, left, right):
    return pl.pallas_call(
        response_kernel,
        out_shape=jax.ShapeDtypeStruct((NAUX, NAUX), jnp.bfloat16),
        grid=(OWN,),
        in_specs=[
            pl.BlockSpec((NAUX, 1), lambda j: (0, 0)),
            pl.BlockSpec((GRP, PAIR, 1, AUX, SEC), lambda j: (0, 0, j, 0, 0)),
            pl.BlockSpec((PAIR, 1, AUX, NORB), lambda j: (0, j, 0, 0)),
        ],
        out_specs=pl.BlockSpec((NAUX, NAUX), lambda j: (0, 0)),
        scratch_shapes=[pltpu.VMEM((NAUX, NAUX), jnp.float32)],
        name="partial_response",
    )(order, left, right)


def per_device(
    three_center, virt_density, occ_density, tensor_mask, virt_mask, occ_mask, panel_order
):
    pair, grp = lax.axis_index("pair"), lax.axis_index("grp")
    tensor = three_center.reshape(AUX * SEC, NORB)
    table_rows = tensor_mask.reshape(-1, NORB // BLK)
    table = (pair * AUX // BLK) * (NORB // BLK) + grp
    place = jnp.stack([pair % 2, table]).astype(jnp.int32)

    shard = jnp.concatenate([virt_density.T, occ_density.T], axis=0)
    own = lax.all_to_all(
        jnp.broadcast_to(shard[None], (CHIPS, 2 * COLS, NORB)),
        "pair",
        0,
        0,
        axis_index_groups=SAME_CORE,
        tiled=True,
    )
    other = lax.ppermute(own, "pair", PARTNER)

    half = half_transform(place, virt_mask, table_rows, own, other, tensor)
    half = half.reshape(GRP * PAIR, OWN * AUX, SEC)
    left = lax.all_to_all(half, ("grp", "pair"), 0, 0, tiled=True)
    turned = turn_transform(place, occ_mask, table_rows, own, other, tensor)
    turned = turned.reshape(PAIR, OWN * AUX, NORB)
    right = lax.all_to_all(turned, "pair", 0, 0, tiled=True)

    order = panel_order.reshape(GRP, PAIR, 2).transpose(1, 0, 2).reshape(NAUX, 1)
    product = partial_response(
        order,
        left.reshape(GRP, PAIR, OWN, AUX, SEC),
        right.reshape(PAIR, OWN, AUX, NORB),
    )
    rows = lax.all_to_all(product.reshape(PAIR, AUX, NAUX), "pair", 0, 0, tiled=True)
    rows = jnp.sum(rows.astype(jnp.float32), axis=0).reshape(GRP, 2, NAUX)
    rows = lax.all_to_all(rows, "grp", 0, 0, tiled=True)
    return jnp.sum(rows, axis=0)


def solution(mesh):
    placed = (P("pair", "grp", None), P(None, "pair"), P(None, "pair"), P(), P(), P(), P())
    return jax.shard_map(
        per_device, mesh=mesh, in_specs=placed, out_specs=P(("grp", "pair"), None), check_vma=False
    )
```

```python
import functools

import jax
import jax.numpy as jnp
from jax import lax
from jax.experimental import pallas as pl
from jax.experimental.pallas import tpu as pltpu
from jax.sharding import PartitionSpec as P

NAUX = 512
NORB = 1024
BLK = 128
GRP = 8
PAIR = 32
AUX = NAUX // PAIR
SEC = NORB // GRP
COLS = NORB // PAIR
CHIPS = PAIR // 2
OWN = SEC // PAIR

SAME_CORE = [[core + 2 * chip for chip in range(CHIPS)] for core in range(2)]
PARTNER = [(i, i ^ 1) for i in range(PAIR)]
NT = (((1,), (1,)), ((), ()))
SMEM = pl.BlockSpec(memory_space=pltpu.SMEM)


def masked_rows(rows, keep):
    parts = []
    for b in range(NORB // BLK):
        part = rows[:, b * BLK : (b + 1) * BLK]
        parts.append(jnp.where(keep(b) != 0, part, jnp.zeros_like(part)))
    return jnp.concatenate(parts, axis=1)


S_TILE = 256


def half_kernel(place, virt_mask, tensor_mask, own, other, tensor, out, virt):
    core, table = place[0], place[1]
    tile = pl.program_id(0)
    chips = S_TILE // (2 * COLS)
    for c in range(chips):
        block = (tile * S_TILE + c * 2 * COLS) // BLK

        def keep(b):
            return virt_mask[b, block] * tensor_mask[table, b]

        mine = pl.multiple_of((2 * c + core) * COLS, COLS)
        theirs = pl.multiple_of((2 * c + 1 - core) * COLS, COLS)
        virt[pl.ds(mine, COLS), :] = masked_rows(own[c], keep)
        virt[pl.ds(theirs, COLS), :] = masked_rows(other[c], keep)
    half = lax.dot_general(virt[...], tensor[...], NT, preferred_element_type=jnp.float32)
    half = half.astype(jnp.bfloat16)
    by_aux = jnp.stack([half[:, a * SEC : (a + 1) * SEC] for a in range(AUX)], axis=0)
    out[...] = jnp.swapaxes(by_aux, 0, 1)


def half_transform(place, virt_mask, tensor_mask, own, other, tensor):
    chips = S_TILE // (2 * COLS)
    return pl.pallas_call(
        half_kernel,
        out_shape=jax.ShapeDtypeStruct((NORB, AUX, SEC), jnp.bfloat16),
        grid=(NORB // S_TILE,),
        in_specs=[
            SMEM,
            SMEM,
            SMEM,
            pl.BlockSpec((chips, COLS, NORB), lambda i: (i, 0, 0)),
            pl.BlockSpec((chips, COLS, NORB), lambda i: (i, 0, 0)),
            pl.BlockSpec((AUX * SEC, NORB), lambda i: (0, 0)),
        ],
        out_specs=pl.BlockSpec((S_TILE, AUX, SEC), lambda i: (i, 0, 0)),
        scratch_shapes=[pltpu.VMEM((S_TILE, NORB), jnp.bfloat16)],
        name="half_transform",
    )(place, virt_mask, tensor_mask, own, other, tensor)


M_TILE = 256


def turn_kernel(place, occ_mask, tensor_mask, own, other, tensor, *refs):
    outs, (occ, by_row) = refs[:PAIR], refs[PAIR:]
    core, table, pair = place[0], place[1], place[2]
    tile = pl.program_id(0)

    for c in range(CHIPS):
        block = c * 2 * COLS // BLK
        for rows, at in ((own, 2 * c + core), (other, 2 * c + 1 - core)):
            parts = []
            for b in range(M_TILE // BLK):
                part = rows[c, :, b * BLK : (b + 1) * BLK]
                live = occ_mask[tile * (M_TILE // BLK) + b, block] * tensor_mask[table, block]
                parts.append(jnp.where(live != 0, part, jnp.zeros_like(part)))
            occ[pl.ds(pl.multiple_of(at * COLS, COLS), COLS), :] = jnp.concatenate(parts, axis=1)

    turned = lax.dot_general(
        tensor[...], occ[...], (((1,), (0,)), ((), ())), preferred_element_type=jnp.float32
    )
    turned = turned.astype(jnp.bfloat16).reshape(AUX, SEC, M_TILE)
    by_row[...] = jnp.swapaxes(turned, 0, 1)
    for d, out in enumerate(outs):
        out[...] = by_row[pl.ds((pair ^ d) * OWN, OWN)]


def turn_transform(place, occ_mask, tensor_mask, own, other, tensor):
    return pl.pallas_call(
        turn_kernel,
        out_shape=[jax.ShapeDtypeStruct((OWN, AUX, NORB), jnp.bfloat16)] * PAIR,
        grid=(NORB // M_TILE,),
        in_specs=[
            SMEM,
            SMEM,
            SMEM,
            pl.BlockSpec((CHIPS, COLS, M_TILE), lambda i: (0, 1, i)),
            pl.BlockSpec((CHIPS, COLS, M_TILE), lambda i: (0, 1, i)),
            pl.BlockSpec((AUX * SEC, NORB), lambda i: (0, 0)),
        ],
        out_specs=[pl.BlockSpec((OWN, AUX, M_TILE), lambda i: (0, 0, i))] * PAIR,
        scratch_shapes=[
            pltpu.VMEM((NORB, M_TILE), jnp.bfloat16),
            pltpu.VMEM((SEC, AUX, M_TILE), jnp.bfloat16),
        ],
        name="turn_transform",
    )(place, occ_mask, tensor_mask, own, other, tensor)


def response_kernel(place, order, left, *refs):
    rights, (out, total, rhs) = refs[:PAIR], refs[PAIR:]
    pair = place[2]
    step = pl.program_id(0)
    for d, right in enumerate(rights):
        rhs[pl.ds(pl.multiple_of((pair ^ d) * AUX, AUX), AUX), :] = right[0]
    lhs = jnp.concatenate([left[g, :, 0].reshape(NAUX, SEC) for g in range(GRP)], axis=1)
    part = lax.dot_general(lhs, rhs[...], NT, preferred_element_type=jnp.float32)

    @pl.when(step == 0)
    def _():
        total[...] = part

    @pl.when(step > 0)
    def _():
        total[...] += part

    @pl.when(step == pl.num_programs(0) - 1)
    def _():
        rounded = (total[...] * (1.0 / NORB)).astype(jnp.bfloat16)
        columns = lax.broadcasted_iota(jnp.int32, (NAUX, NAUX), 1)
        pick = (order[...] == columns).astype(jnp.float32).astype(jnp.bfloat16)
        picked = jnp.dot(pick, rounded, preferred_element_type=jnp.float32)
        out[...] = picked.astype(jnp.bfloat16)


def partial_response(place, order, left, rights):
    return pl.pallas_call(
        response_kernel,
        out_shape=jax.ShapeDtypeStruct((NAUX, NAUX), jnp.bfloat16),
        grid=(OWN,),
        in_specs=[
            SMEM,
            pl.BlockSpec((NAUX, 1), lambda j: (0, 0)),
            pl.BlockSpec((GRP, PAIR, 1, AUX, SEC), lambda j: (0, 0, j, 0, 0)),
        ]
        + [pl.BlockSpec((1, AUX, NORB), lambda j: (j, 0, 0))] * PAIR,
        out_specs=pl.BlockSpec((NAUX, NAUX), lambda j: (0, 0)),
        scratch_shapes=[
            pltpu.VMEM((NAUX, NAUX), jnp.float32),
            pltpu.VMEM((NAUX, NORB), jnp.bfloat16),
        ],
        name="partial_response",
    )(place, order, left, *rights)


def per_device(
    three_center, virt_density, occ_density, tensor_mask, virt_mask, occ_mask, panel_order
):
    pair, grp = lax.axis_index("pair"), lax.axis_index("grp")
    tensor = three_center.reshape(AUX * SEC, NORB)
    table_rows = tensor_mask.reshape(-1, NORB // BLK)
    table = (pair * AUX // BLK) * (NORB // BLK) + grp
    place = jnp.stack([pair % 2, table, pair]).astype(jnp.int32)

    shard = jnp.concatenate([virt_density.T, occ_density.T], axis=0)
    own = lax.all_to_all(
        jnp.broadcast_to(shard[None], (CHIPS, 2 * COLS, NORB)),
        "pair",
        0,
        0,
        axis_index_groups=SAME_CORE,
        tiled=True,
    )
    other = lax.ppermute(own, "pair", PARTNER)

    half = half_transform(place, virt_mask, table_rows, own, other, tensor)
    half = half.reshape(GRP * PAIR, OWN * AUX, SEC)
    left = lax.all_to_all(half, ("grp", "pair"), 0, 0, tiled=True)
    turned = turn_transform(place, occ_mask, table_rows, own, other, tensor)
    rights = [turned[0]]
    for d in range(1, PAIR):
        rights.append(lax.ppermute(turned[d], "pair", [(i, i ^ d) for i in range(PAIR)]))

    order = panel_order.reshape(GRP, PAIR, 2).transpose(1, 0, 2).reshape(NAUX, 1)
    product = partial_response(place, order, left.reshape(GRP, PAIR, OWN, AUX, SEC), rights)
    rows = lax.all_to_all(product.reshape(PAIR, AUX, NAUX), "pair", 0, 0, tiled=True)
    rows = jnp.sum(rows.astype(jnp.float32), axis=0).reshape(GRP, 2, NAUX)
    rows = lax.all_to_all(rows, "grp", 0, 0, tiled=True)
    return jnp.sum(rows, axis=0)


def solution(mesh):
    placed = (P("pair", "grp", None), P(None, "pair"), P(None, "pair"), P(), P(), P(), P())
    return jax.shard_map(
        per_device, mesh=mesh, in_specs=placed, out_specs=P(("grp", "pair"), None), check_vma=False
    )
```

```python
import jax
import jax.numpy as jnp
from jax import lax
from jax.experimental import pallas as pl
from jax.experimental.pallas import tpu as pltpu
from jax.sharding import PartitionSpec as P

NAUX = 512
NORB = 1024
BLK = 128
GRP = 8
PAIR = 32
AUX = NAUX // PAIR
SEC = NORB // GRP
COLS = NORB // PAIR
CHIPS = PAIR // 2
OWN = SEC // PAIR

SAME_CORE = [[core + 2 * chip for chip in range(CHIPS)] for core in range(2)]
GATHERED = [4 * x + y for y in range(4) for x in range(4)]
OFFSETS = [
    (2, 2), (0, 2), (1, 3), (3, 1), (1, 2), (2, 0), (0, 1), (3, 2),
    (1, 1), (3, 3), (2, 1), (0, 3), (2, 3), (1, 0), (3, 0),
]
SHIFTS = [8 * x + 2 * y + core for x, y in OFFSETS for core in range(2)] + [1]
ORDER = [0] + SHIFTS
NT = (((1,), (1,)), ((), ()))
SMEM = pl.BlockSpec(memory_space=pltpu.SMEM)


def masked_rows(rows, keep):
    parts = []
    for b in range(NORB // BLK):
        part = rows[:, b * BLK : (b + 1) * BLK]
        parts.append(jnp.where(keep(b) != 0, part, jnp.zeros_like(part)))
    return jnp.concatenate(parts, axis=1)


S_TILE = 256


def half_kernel(place, virt_mask, tensor_mask, own, other, tensor, out, virt):
    core, table = place[0], place[1]
    tile = pl.program_id(0)
    chips = S_TILE // (2 * COLS)
    for c in range(chips):
        block = (tile * S_TILE + c * 2 * COLS) // BLK

        def keep(b):
            return virt_mask[b, block] * tensor_mask[table, b]

        mine = pl.multiple_of((2 * c + core) * COLS, COLS)
        theirs = pl.multiple_of((2 * c + 1 - core) * COLS, COLS)
        virt[pl.ds(mine, COLS), :] = masked_rows(own[c], keep)
        virt[pl.ds(theirs, COLS), :] = masked_rows(other[c], keep)
    half = lax.dot_general(virt[...], tensor[...], NT, preferred_element_type=jnp.float32)
    half = half.astype(jnp.bfloat16)
    by_aux = jnp.stack([half[:, a * SEC : (a + 1) * SEC] for a in range(AUX)], axis=0)
    out[...] = jnp.swapaxes(by_aux, 0, 1)


def half_transform(place, virt_mask, tensor_mask, own, other, tensor):
    chips = S_TILE // (2 * COLS)
    return pl.pallas_call(
        half_kernel,
        out_shape=jax.ShapeDtypeStruct((NORB, AUX, SEC), jnp.bfloat16),
        grid=(NORB // S_TILE,),
        in_specs=[
            SMEM,
            SMEM,
            SMEM,
            pl.BlockSpec((chips, COLS, NORB), lambda i: (i, 0, 0)),
            pl.BlockSpec((chips, COLS, NORB), lambda i: (i, 0, 0)),
            pl.BlockSpec((AUX * SEC, NORB), lambda i: (0, 0)),
        ],
        out_specs=pl.BlockSpec((S_TILE, AUX, SEC), lambda i: (i, 0, 0)),
        scratch_shapes=[pltpu.VMEM((S_TILE, NORB), jnp.bfloat16)],
        name="half_transform",
    )(place, virt_mask, tensor_mask, own, other, tensor)


M_TILE = 256


def turn_kernel(place, occ_mask, tensor_mask, own, other, tensor, *refs):
    outs, (occ, by_row) = refs[:PAIR], refs[PAIR:]
    core, table, pair = place[0], place[1], place[2]
    tile = pl.program_id(0)

    for c in range(CHIPS):
        chip = pair // 2 ^ GATHERED[c]
        block = chip * 2 * COLS // BLK
        for rows, at in ((own, 2 * chip + core), (other, 2 * chip + 1 - core)):
            parts = []
            for b in range(M_TILE // BLK):
                part = rows[c, :, b * BLK : (b + 1) * BLK]
                live = occ_mask[tile * (M_TILE // BLK) + b, block] * tensor_mask[table, block]
                parts.append(jnp.where(live != 0, part, jnp.zeros_like(part)))
            occ[pl.ds(pl.multiple_of(at * COLS, COLS), COLS), :] = jnp.concatenate(parts, axis=1)

    turned = lax.dot_general(
        tensor[...], occ[...], (((1,), (0,)), ((), ())), preferred_element_type=jnp.float32
    )
    turned = turned.astype(jnp.bfloat16).reshape(AUX, SEC, M_TILE)
    by_row[...] = jnp.swapaxes(turned, 0, 1)
    for d, out in enumerate(outs):
        out[...] = by_row[pl.ds((pair ^ d) * OWN, OWN)]


def turn_transform(place, occ_mask, tensor_mask, own, other, tensor):
    return pl.pallas_call(
        turn_kernel,
        out_shape=[jax.ShapeDtypeStruct((OWN, AUX, NORB), jnp.bfloat16)] * PAIR,
        grid=(NORB // M_TILE,),
        in_specs=[
            SMEM,
            SMEM,
            SMEM,
            pl.BlockSpec((CHIPS, COLS, M_TILE), lambda i: (0, 0, i)),
            pl.BlockSpec((CHIPS, COLS, M_TILE), lambda i: (0, 0, i)),
            pl.BlockSpec((AUX * SEC, NORB), lambda i: (0, 0)),
        ],
        out_specs=[pl.BlockSpec((OWN, AUX, M_TILE), lambda i: (0, 0, i))] * PAIR,
        scratch_shapes=[
            pltpu.VMEM((NORB, M_TILE), jnp.bfloat16),
            pltpu.VMEM((SEC, AUX, M_TILE), jnp.bfloat16),
        ],
        name="turn_transform",
    )(place, occ_mask, tensor_mask, own, other, tensor)


def response_kernel(place, order, left, *refs):
    rights, (out, total, rhs) = refs[:PAIR], refs[PAIR:]
    pair = place[2]
    step = pl.program_id(0)
    for d, right in zip(ORDER, rights):
        rhs[pl.ds(pl.multiple_of((pair ^ d) * AUX, AUX), AUX), :] = right[0]
    lhs = jnp.concatenate([left[g, :, 0].reshape(NAUX, SEC) for g in range(GRP)], axis=1)
    part = lax.dot_general(lhs, rhs[...], NT, preferred_element_type=jnp.float32)

    @pl.when(step == 0)
    def _():
        total[...] = part

    @pl.when(step > 0)
    def _():
        total[...] += part

    @pl.when(step == pl.num_programs(0) - 1)
    def _():
        rounded = (total[...] * (1.0 / NORB)).astype(jnp.bfloat16)
        columns = lax.broadcasted_iota(jnp.int32, (NAUX, NAUX), 1)
        pick = (order[...] == columns).astype(jnp.float32).astype(jnp.bfloat16)
        picked = jnp.dot(pick, rounded, preferred_element_type=jnp.float32)
        out[...] = picked.astype(jnp.bfloat16)


def partial_response(place, order, left, rights):
    return pl.pallas_call(
        response_kernel,
        out_shape=jax.ShapeDtypeStruct((NAUX, NAUX), jnp.bfloat16),
        grid=(OWN,),
        in_specs=[
            SMEM,
            pl.BlockSpec((NAUX, 1), lambda j: (0, 0)),
            pl.BlockSpec((GRP, PAIR, 1, AUX, SEC), lambda j: (0, 0, j, 0, 0)),
        ]
        + [pl.BlockSpec((1, AUX, NORB), lambda j: (j, 0, 0))] * PAIR,
        out_specs=pl.BlockSpec((NAUX, NAUX), lambda j: (0, 0)),
        scratch_shapes=[
            pltpu.VMEM((NAUX, NAUX), jnp.float32),
            pltpu.VMEM((NAUX, NORB), jnp.bfloat16),
        ],
        name="partial_response",
    )(place, order, left, *rights)


def exchange(array, d):
    return lax.ppermute(array, "pair", [(i, i ^ d) for i in range(PAIR)])


def per_device(
    three_center, virt_density, occ_density, tensor_mask, virt_mask, occ_mask, panel_order
):
    pair, grp = lax.axis_index("pair"), lax.axis_index("grp")
    tensor = three_center.reshape(AUX * SEC, NORB)
    table_rows = tensor_mask.reshape(-1, NORB // BLK)
    table = (pair * AUX // BLK) * (NORB // BLK) + grp
    place = jnp.stack([pair % 2, table, pair]).astype(jnp.int32)

    virt = lax.all_to_all(
        jnp.broadcast_to(virt_density.T[None], (CHIPS, COLS, NORB)),
        "pair",
        0,
        0,
        axis_index_groups=SAME_CORE,
        tiled=True,
    )
    virt_other = exchange(virt, 1)
    occ = occ_density.T[None]
    parts = [exchange(occ, 8 * k) for k in (1, 2, 3)]
    occ = jnp.concatenate([occ] + parts, axis=0)
    parts = [exchange(occ, 2 * k) for k in (1, 2, 3)]
    occ = jnp.concatenate([occ] + parts, axis=0)
    occ_other = exchange(occ, 1)

    half = half_transform(place, virt_mask, table_rows, virt, virt_other, tensor)
    half = half.reshape(GRP * PAIR, OWN * AUX, SEC)
    left = lax.all_to_all(half, ("grp", "pair"), 0, 0, tiled=True)
    turned = turn_transform(place, occ_mask, table_rows, occ, occ_other, tensor)
    rights = [turned[0]]
    for d in ORDER[1:]:
        rights.append(exchange(turned[d], d))

    order = panel_order.reshape(GRP, PAIR, 2).transpose(1, 0, 2).reshape(NAUX, 1)
    product = partial_response(place, order, left.reshape(GRP, PAIR, OWN, AUX, SEC), rights)
    rows = lax.all_to_all(product.reshape(PAIR, AUX, NAUX), "pair", 0, 0, tiled=True)
    rows = jnp.sum(rows.astype(jnp.float32), axis=0).reshape(GRP, 2, NAUX)
    rows = lax.all_to_all(rows, "grp", 0, 0, tiled=True)
    return jnp.sum(rows, axis=0)


def solution(mesh):
    placed = (P("pair", "grp", None), P(None, "pair"), P(None, "pair"), P(), P(), P(), P())
    return jax.shard_map(
        per_device, mesh=mesh, in_specs=placed, out_specs=P(("grp", "pair"), None), check_vma=False
    )
```
